128 devices in a mesh: tm: 8 (over x, z_hi), pts: 16 (over z_lo, y, core).
Axes of the slice: x: 4, y: 4, z: 4 (z_hi: 2, z_lo: 2; z = z_hi * 2 + z_lo), core: 2. Of those that a mesh axis runs over, the one named last changes fastest.
Arguments:
- psi_rows: bfloat16 [512, 6144], replicated, may hold values from -1.1953125 to 1.1953125
- psi_cols: bfloat16 [6144, 16384], P(None, 'pts'), may hold values from -1.1953125 to 1.1953125
- psi_slab: bfloat16 [1024, 1024], replicated, may hold values from -1.1953125 to 1.1953125
- occ_depth: float32 [1024], replicated, may hold values from 0.05 to 2
- virt_height: float32 [5120], replicated, may hold values from 0.05 to 2
- coulomb: bfloat16 [16384, 1024], P('pts'), may hold values from -0.046875 to 0.046875
Outputs:
- sigma: float32 [512, 16, 1024], P('pts', 'tm')
The draws below stay inside these ranges and needn't reach their ends.
All inputs are finite; a program needn't handle non-finite values.
Results may differ from the reference program's by a relative error of at most 0.0065.
Values may be sent and summed in bfloat16 or wider, within the bound.
A program may use at most 128 MiB of HBM per device.

```python
import math
import jax
import jax.numpy as jnp
from jax import lax

ROWS = 512
POINTS = 16384
NOCC = 1024
NVIRT = 5120
ORBITALS = 6144
SLAB = 1024
TIMES = 16


def levels(stream_key, shape, split, least, largest):
    level = 1.0
    for position, shards_of in split:
        draws = jax.random.uniform(jax.random.fold_in(jax.random.fold_in(stream_key, 6), position), (shards_of,), jnp.float32, least / len(split), largest / len(split))
        level = level * jnp.repeat(jnp.exp(draws), shape[position] // shards_of).reshape((-1,) + (1,) * (len(shape) - 1 - position))
    return level


def scatter_about(stream_key, dims, width, bound, shards=(), kind=jnp.bfloat16):
    drawn = jax.random.normal(stream_key, dims, jnp.float32) * width
    if len(shards) > 0:
        drawn = levels(stream_key, dims, shards, -0.22, 0.18) * drawn
    return jnp.clip(drawn, min=-bound, max=bound).astype(kind)


def setup_inputs(seed: int = 0) -> dict:
    arg_keys = jax.random.split(jax.random.key(seed), 7)
    psi_rows = scatter_about(arg_keys[0], (ROWS, ORBITALS), 0.2, 1.1953125)
    psi_cols = scatter_about(arg_keys[1], (ORBITALS, POINTS), 0.2, 1.1953125, ((1, 16),))
    psi_slab = scatter_about(arg_keys[2], (NOCC, SLAB), 0.2, 1.1953125)
    occ_depth = jnp.clip(jnp.exp(jax.random.uniform(arg_keys[3], (NOCC,), jnp.float32, math.log(0.05), math.log(2.0))), 0.05, 2.0)
    virt_height = jnp.clip(jnp.exp(jax.random.uniform(arg_keys[4], (NVIRT,), jnp.float32, math.log(0.05), math.log(2.0))), 0.05, 2.0)
    coulomb = scatter_about(arg_keys[5], (POINTS, SLAB), POINTS ** -0.5, 0.046875, ((0, 16),))
    return dict(psi_rows=psi_rows, psi_cols=psi_cols, psi_slab=psi_slab, occ_depth=occ_depth, virt_height=virt_height, coulomb=coulomb)


TIME_SPAN = 8.0
FREQ_SPAN = 8.0

def transform_tables():
    steps = jnp.arange(TIMES, dtype=jnp.float32) + 0.5
    fraction = steps / TIMES
    times_grid = TIME_SPAN * fraction * fraction
    time_weight = TIME_SPAN * 2.0 * fraction / TIMES
    frequency = FREQ_SPAN * fraction * fraction
    freq_weight = FREQ_SPAN * 2.0 * fraction / TIMES
    forward = time_weight[None, :] * jnp.cos(frequency[:, None] * times_grid[None, :])
    backward = 2.0 / math.pi * freq_weight[None, :] * jnp.cos(times_grid[:, None] * frequency[None, :])
    return (times_grid, forward, backward)

def reference(psi_rows, psi_cols, psi_slab, occ_depth, virt_height, coulomb):
    times_grid, forward, backward = transform_tables()
    occ_cols = psi_cols[:NOCC]
    virt_cols = psi_cols[NOCC:]
    block = min(ROWS, 64)

    def row_block(block_rows):
        occ_rows = block_rows[:, :NOCC].astype(jnp.float32)
        virt_rows = block_rows[:, NOCC:].astype(jnp.float32)

        def one_time(moment):
            scaled_occ = (occ_rows * jnp.exp(-occ_depth * moment)[None, :]).astype(jnp.bfloat16)
            scaled_virt = (virt_rows * jnp.exp(-virt_height * moment)[None, :]).astype(jnp.bfloat16)
            green_occ = jnp.dot(scaled_occ, occ_cols, preferred_element_type=jnp.float32)
            green_virt = jnp.dot(scaled_virt, virt_cols, preferred_element_type=jnp.float32)
            chi_part = (green_occ * green_virt).astype(jnp.bfloat16)
            green_slab = jnp.dot(scaled_occ, psi_slab, preferred_element_type=jnp.float32)
            return (chi_part, green_slab)
        chi_time, green_slab = lax.map(one_time, times_grid)
        chi_freq = jnp.einsum('wt,tbp->wbp', forward, chi_time.astype(jnp.float32), precision=lax.Precision.HIGHEST).astype(jnp.bfloat16)
        screened = lax.map(lambda part: jnp.dot(part, coulomb, preferred_element_type=jnp.float32), chi_freq)
        resummed = screened / jnp.sqrt(1.0 + screened * screened)
        screened_time = jnp.einsum('tw,wbq->tbq', backward, resummed, precision=lax.Precision.HIGHEST)
        return jnp.transpose(green_slab * screened_time, (1, 0, 2))
    result = lax.map(row_block, psi_rows.reshape(ROWS // block, block, ORBITALS))
    return result.reshape(ROWS, TIMES, SLAB)
```

```python
import math

import jax
import jax.numpy as jnp
from jax import lax
from jax.sharding import PartitionSpec as P

NOCC = 1024
TIMES = 16


TIME_SPAN = 8.0
FREQ_SPAN = 8.0


def transform_tables():
    steps = jnp.arange(TIMES, dtype=jnp.float32) + 0.5
    fraction = steps / TIMES
    times_grid = TIME_SPAN * fraction * fraction
    time_weight = TIME_SPAN * 2.0 * fraction / TIMES
    frequency = FREQ_SPAN * fraction * fraction
    freq_weight = FREQ_SPAN * 2.0 * fraction / TIMES
    forward = time_weight[None, :] * jnp.cos(frequency[:, None] * times_grid[None, :])
    backward = (
        2.0 / math.pi * freq_weight[None, :] * jnp.cos(times_grid[:, None] * frequency[None, :])
    )
    return (times_grid, forward, backward)


def per_device(psi_rows, psi_cols, psi_slab, occ_depth, virt_height, coulomb):
    teams = lax.axis_size("tm")
    owners = lax.axis_size("pts")
    local_times = TIMES // teams
    time_rank = lax.axis_index("tm")
    point_rank = lax.axis_index("pts")
    all_rows, orbitals = psi_rows.shape
    local_rows = all_rows // owners
    share = local_rows // teams
    points = psi_cols.shape[1]
    slab = coulomb.shape[1]
    times_grid, forward, backward = transform_tables()

    dealt = psi_rows.reshape(owners, teams, share, orbitals)
    dealt = lax.dynamic_index_in_dim(dealt, time_rank, 1, keepdims=False)
    dealt = dealt.reshape(owners * share, orbitals).astype(jnp.float32)
    heights = jnp.concatenate([occ_depth, virt_height])
    decay = jnp.exp(-heights[None, :] * times_grid[:, None])
    scaled = (dealt[:, None, :] * decay[None, :, :]).astype(jnp.bfloat16)
    scaled = scaled.reshape(owners * share * TIMES, orbitals)
    green_occ = jnp.dot(scaled[:, :NOCC], psi_cols[:NOCC], preferred_element_type=jnp.float32)
    green_virt = jnp.dot(scaled[:, NOCC:], psi_cols[NOCC:], preferred_element_type=jnp.float32)
    chi_time = (green_occ * green_virt).astype(jnp.bfloat16)
    partial = jnp.dot(chi_time, coulomb, preferred_element_type=jnp.float32)
    summed = lax.psum_scatter(partial, "pts", scatter_dimension=0, tiled=True)
    summed = summed.reshape(share, TIMES, slab)

    screened = jnp.einsum("wt,rtq->rwq", forward, summed, precision=lax.Precision.HIGHEST)
    resummed = screened / jnp.sqrt(1.0 + screened * screened)
    by_time = jnp.einsum("tw,rwq->rtq", backward, resummed, precision=lax.Precision.HIGHEST)
    screened_time = lax.all_to_all(by_time, "tm", split_axis=1, concat_axis=0, tiled=True)

    mine = lax.dynamic_slice_in_dim(psi_rows[:, :NOCC], point_rank * local_rows, local_rows, 0)
    my_decay = lax.dynamic_slice_in_dim(decay[:, :NOCC], time_rank * local_times, local_times, 0)
    mine = (mine.astype(jnp.float32)[:, None, :] * my_decay[None]).astype(jnp.bfloat16)
    green_slab = jnp.einsum("rti,iq->rtq", mine, psi_slab, preferred_element_type=jnp.float32)
    return green_slab * screened_time


def solution(mesh):
    in_specs = (P(), P(None, "pts"), P(), P(), P(), P("pts", None))
    out_specs = P("pts", "tm", None)
    return jax.shard_map(
        per_device, mesh=mesh, in_specs=in_specs, out_specs=out_specs, check_vma=False
    )
```

```python
import functools
import math

import jax
import jax.numpy as jnp
import ml_dtypes
import numpy as np
from jax import lax
from jax.experimental import pallas as pl
from jax.experimental.pallas import tpu as pltpu
from jax.sharding import PartitionSpec as P

MESH = pl.DeviceIdType.MESH
NOCC = 1024
TIMES = 16
TIME_SPAN = 8.0
FREQ_SPAN = 8.0
TILE = 256
CORES = 2


def transform_tables():
    fraction = (np.arange(TIMES, dtype=np.float64) + 0.5) / TIMES
    times_grid = TIME_SPAN * fraction * fraction
    time_weight = TIME_SPAN * 2.0 * fraction / TIMES
    frequency = FREQ_SPAN * fraction * fraction
    freq_weight = FREQ_SPAN * 2.0 * fraction / TIMES
    forward = time_weight[None, :] * np.cos(frequency[:, None] * times_grid[None, :])
    backward = (
        2.0 / math.pi * freq_weight[None, :] * np.cos(times_grid[:, None] * frequency[None, :])
    )
    return forward.astype(np.float32), backward.astype(np.float32)


def forward_blocks(groups):
    forward, _ = transform_tables()
    whole = np.kron(np.eye(groups, dtype=np.float32), forward)
    high = whole.astype(ml_dtypes.bfloat16)
    low = (whole - high.astype(np.float32)).astype(ml_dtypes.bfloat16)
    return np.stack([high, low])


def kernel(
    sizes,
    rows_hbm, cols_hbm, slab_hbm, occ_ref, virt_ref, coulomb_hbm, forward_ref, backward_ref,
    out_hbm,
    raw, rows, decay, scaled0, scaled1, own_scaled, cols, coulomb, slab, chi, freq,
    half, half_send, half_recv, sum_send, sum_recv, mine, green, sigma,
    raw_sem, cols_sem, misc_sem, half_ssem, half_rsem, sum_ssem, sum_rsem, out_ssem, out_rsem,
    own_sem,
):
    teams, zs, ys, share, band = sizes
    owners = zs * ys * CORES
    peers = zs * ys
    tiles = cols.shape[0]
    orbitals = decay.shape[1]
    chunk = owners * TIMES
    halves = chunk // CORES
    strip = orbitals // tiles
    t = lax.axis_index("tm")
    p = lax.axis_index("pts")
    core = lax.rem(p, CORES)
    y = lax.rem(p // CORES, ys)
    z = p // (CORES * ys)
    partner = (t, p + 1 - 2 * core)

    def peer(h):
        return lax.rem(z + h // ys, zs), lax.rem(y + h % ys, ys)

    def peer_id(h):
        pz, py = peer(h)
        return (t, (pz * ys + py) * CORES + core)

    def team_id(d):
        return (lax.rem(t + d, teams), p)

    barrier = pltpu.get_barrier_semaphore()
    pl.semaphore_signal(barrier, inc=1, device_id=partner, device_id_type=MESH)
    for h in range(1, peers):
        pl.semaphore_signal(barrier, inc=1, device_id=peer_id(h), device_id_type=MESH)
    for d in range(1, teams):
        pl.semaphore_signal(barrier, inc=1, device_id=team_id(d), device_id_type=MESH)

    def raw_copy(g):
        owner = (g % peers) * CORES + g // peers
        first = pl.multiple_of(owner * (teams * share) + (t * share) // band * band, band)
        return pltpu.make_async_copy(
            rows_hbm.at[pl.ds(first, band)], raw.at[pl.ds(g * band, band)], raw_sem.at[g]
        )

    def cols_copy(n):
        return pltpu.make_async_copy(
            cols_hbm.at[:, pl.ds(pl.multiple_of(n * TILE, TILE), TILE)], cols.at[n], cols_sem.at[n]
        )

    for g in range(owners):
        raw_copy(g).start()
    for n in range(tiles):
        cols_copy(n).start()
    coulomb_copy = pltpu.make_async_copy(coulomb_hbm, coulomb, misc_sem.at[0])
    slab_copy = pltpu.make_async_copy(slab_hbm, slab, misc_sem.at[1])
    coulomb_copy.start()
    slab_copy.start()

    fraction = (lax.broadcasted_iota(jnp.int32, (TIMES, 1), 0).astype(jnp.float32) + 0.5) / TIMES
    moments = TIME_SPAN * fraction * fraction
    decay[:, :NOCC] = jnp.exp(-occ_ref[...] * moments)
    decay[:, NOCC:] = jnp.exp(-virt_ref[...] * moments)
    for g in range(owners):
        raw_copy(g).wait()
    rows[...] = raw[...].astype(jnp.float32)
    inner = lax.rem(t * share, band)

    def scale(target, s, n):
        where = pl.ds(pl.multiple_of(n * strip, strip), strip)
        factor = decay[:, where]
        for g in range(owners):
            row = rows[pl.ds(g * band + inner + s, 1), where]
            target[g * TIMES : (g + 1) * TIMES, where] = (row * factor).astype(jnp.bfloat16)

    scaled = (scaled0, scaled1)
    own_group = core * peers + z * ys + y
    for s in range(share):
        row = rows[pl.ds(own_group * band + inner + s, 1), :NOCC]
        own_scaled[s * TIMES : (s + 1) * TIMES] = (row * decay[:, :NOCC]).astype(jnp.bfloat16)

    def first_scale(n, carry):
        scale(scaled0, 0, n)
        return carry

    lax.fori_loop(0, tiles, first_scale, 0)

    def half_copy(s):
        return pltpu.make_async_remote_copy(
            half_send.at[s], half_recv.at[s], half_ssem.at[s], half_rsem.at[s],
            device_id=partner, device_id_type=MESH,
        )

    def sum_copy(s, h):
        pz, py = peer(h)
        where = pl.ds(pl.multiple_of((pz * ys + py) * TIMES, TIMES), TIMES)
        return pltpu.make_async_remote_copy(
            sum_send.at[s, where], sum_recv.at[s, h - 1], sum_ssem.at[s, h - 1],
            sum_rsem.at[s, h - 1], device_id=peer_id(h), device_id_type=MESH,
        )

    def out_copy(s, d):
        return pltpu.make_async_remote_copy(
            sigma.at[s, lax.rem(t + d, teams)], out_hbm.at[t * share + s],
            out_ssem.at[s, d - 1], out_rsem.at[s, d - 1],
            device_id=team_id(d), device_id_type=MESH,
        )

    def own_copy(s):
        return pltpu.make_async_copy(sigma.at[s, t], out_hbm.at[t * share + s], own_sem.at[s])

    def green_loop(s):
        now, later = scaled[s % 2], scaled[(s + 1) % 2]

        def body(n, carry):
            if s == 0:
                cols_copy(n).wait()
            occ = jnp.dot(now[:, :NOCC], cols[n, :NOCC], preferred_element_type=jnp.float32)
            virt = jnp.dot(now[:, NOCC:], cols[n, NOCC:], preferred_element_type=jnp.float32)
            where = pl.ds(pl.multiple_of(n * TILE, TILE), TILE)
            chi[:, where] = (occ * virt).astype(jnp.bfloat16)
            if s + 1 < share:
                scale(later, s + 1, n)
            return carry

        lax.fori_loop(0, tiles, body, 0)

    def screen(s):
        def to_freq(n, carry):
            where = pl.ds(pl.multiple_of(n * TILE, TILE), TILE)
            part = chi[:, where]
            freq[:, where] = (
                jnp.dot(forward_ref[0], part, preferred_element_type=jnp.float32)
                + jnp.dot(forward_ref[1], part, preferred_element_type=jnp.float32)
            ).astype(jnp.bfloat16)
            return carry

        lax.fori_loop(0, chi.shape[1] // TILE, to_freq, 0)
        if s == 0:
            coulomb_copy.wait()
        theirs = pl.ds(pl.multiple_of((1 - core) * halves, halves), halves)
        ours = pl.ds(pl.multiple_of(core * halves, halves), halves)

        def send_part(n, carry):
            where = pl.ds(pl.multiple_of(n * TILE, TILE), TILE)
            half_send[s, :, where] = jnp.dot(
                freq[theirs, :], coulomb[:, where], preferred_element_type=jnp.float32
            ).astype(jnp.bfloat16)
            return carry

        def keep_part(n, carry):
            where = pl.ds(pl.multiple_of(n * TILE, TILE), TILE)
            half[:, where] = jnp.dot(
                freq[ours, :], coulomb[:, where], preferred_element_type=jnp.float32
            )
            return carry

        lax.fori_loop(0, coulomb.shape[1] // TILE, send_part, 0)
        if s == 0:
            pl.semaphore_wait(barrier, 1 + (peers - 1) + (teams - 1))
        half_copy(s).start()
        lax.fori_loop(0, coulomb.shape[1] // TILE, keep_part, 0)

    def pair_up(s):
        half_copy(s).wait_recv()
        sum_send[s] = (half[...] + half_recv[s].astype(jnp.float32)).astype(jnp.bfloat16)
        for h in range(peers - 1, 0, -1):
            sum_copy(s, h).start()
        here = pl.ds(pl.multiple_of((z * ys + y) * TIMES, TIMES), TIMES)
        mine[s] = half[here, :] + half_recv[s, here, :].astype(jnp.float32)

    def finish(s):
        total = mine[s]
        for h in range(1, peers):
            sum_copy(s, h).wait_recv()
        for h in range(1, peers):
            total = total + sum_recv[s, h - 1].astype(jnp.float32)
        resummed = total / jnp.sqrt(1.0 + total * total)
        by_time = jnp.dot(
            backward_ref[...], resummed, preferred_element_type=jnp.float32,
            precision=lax.Precision.HIGHEST,
        )
        result = by_time * green[s * TIMES : (s + 1) * TIMES]
        local = TIMES // teams
        for d in range(teams):
            sigma[s, d] = result[d * local : (d + 1) * local]
        for d in range(teams - 1, 0, -1):
            out_copy(s, d).start()
        own_copy(s).start()

    for s in range(share):
        green_loop(s)
        if s > 0:
            pair_up(s - 1)
        screen(s)
    pair_up(share - 1)
    slab_copy.wait()
    green[...] = jnp.dot(own_scaled[...], slab[...], preferred_element_type=jnp.float32)
    for s in range(share):
        finish(s)
    for s in range(share):
        half_copy(s).wait_send()
        for h in range(1, peers):
            sum_copy(s, h).wait_send()
        own_copy(s).wait()
        for d in range(1, teams):
            out_copy(s, d).wait_send()
            out_copy(s, d).wait_recv()


def per_device(sizes, psi_rows, psi_cols, psi_slab, occ_depth, virt_height, coulomb):
    teams, zs, ys, share, band = sizes
    owners = zs * ys * CORES
    peers = zs * ys
    orbitals = psi_rows.shape[1]
    points = psi_cols.shape[1]
    slab = psi_slab.shape[1]
    chunk = owners * TIMES
    halves = chunk // CORES
    _, backward = transform_tables()
    bf16, f32 = jnp.bfloat16, jnp.float32
    anywhere = pl.BlockSpec(memory_space=pl.ANY)
    inside = pl.BlockSpec(memory_space=pltpu.VMEM)
    dma = pltpu.SemaphoreType.DMA
    return pl.pallas_call(
        functools.partial(kernel, sizes),
        name="gw_window",
        out_shape=jax.ShapeDtypeStruct((teams * share, TIMES // teams, slab), f32),
        in_specs=[anywhere, anywhere, anywhere, inside, inside, anywhere, inside, inside],
        out_specs=anywhere,
        scratch_shapes=[
            pltpu.VMEM((owners * band, orbitals), bf16),
            pltpu.VMEM((owners * band, orbitals), f32),
            pltpu.VMEM((TIMES, orbitals), f32),
            pltpu.VMEM((chunk, orbitals), bf16),
            pltpu.VMEM((chunk, orbitals), bf16),
            pltpu.VMEM((share * TIMES, NOCC), bf16),
            pltpu.VMEM((points // TILE, orbitals, TILE), bf16),
            pltpu.VMEM((points, slab), bf16),
            pltpu.VMEM((NOCC, slab), bf16),
            pltpu.VMEM((chunk, points), bf16),
            pltpu.VMEM((chunk, points), bf16),
            pltpu.VMEM((halves, slab), f32),
            pltpu.VMEM((share, halves, slab), bf16),
            pltpu.VMEM((share, halves, slab), bf16),
            pltpu.VMEM((share, halves, slab), bf16),
            pltpu.VMEM((share, peers - 1, TIMES, slab), bf16),
            pltpu.VMEM((share, TIMES, slab), f32),
            pltpu.VMEM((share * TIMES, slab), f32),
            pltpu.VMEM((share, teams, TIMES // teams, slab), f32),
            dma((owners,)),
            dma((points // TILE,)),
            dma((2,)),
            dma((share,)),
            dma((share,)),
            dma((share, peers - 1)),
            dma((share, peers - 1)),
            dma((share, teams - 1)),
            dma((share, teams - 1)),
            dma((share,)),
        ],
        compiler_params=pltpu.CompilerParams(
            collective_id=0, has_side_effects=True, vmem_limit_bytes=60 * 1024 * 1024
        ),
    )(
        psi_rows, psi_cols, psi_slab, occ_depth[None], virt_height[None], coulomb,
        jnp.asarray(forward_blocks(owners)), jnp.asarray(backward),
    )


def solution(mesh):
    teams, owners = mesh.shape["tm"], mesh.shape["pts"]
    ys = owners // (2 * CORES)
    sizes = (teams, 2, ys, 512 // (owners * teams), 8)
    in_specs = (P(), P(None, "pts"), P(), P(), P(), P("pts", None))
    out_specs = P("pts", "tm", None)
    return jax.shard_map(
        functools.partial(per_device, sizes),
        mesh=mesh, in_specs=in_specs, out_specs=out_specs, check_vma=False,
    )
```

```python
import functools
import math

import jax
import jax.numpy as jnp
import ml_dtypes
import numpy as np
from jax import lax
from jax.experimental import pallas as pl
from jax.experimental.pallas import tpu as pltpu
from jax.sharding import PartitionSpec as P

MESH = pl.DeviceIdType.MESH
NOCC = 1024
TIMES = 16
TIME_SPAN = 8.0
FREQ_SPAN = 8.0
TILE = 256
CORES = 2


def transform_tables():
    fraction = (np.arange(TIMES, dtype=np.float64) + 0.5) / TIMES
    times_grid = TIME_SPAN * fraction * fraction
    time_weight = TIME_SPAN * 2.0 * fraction / TIMES
    frequency = FREQ_SPAN * fraction * fraction
    freq_weight = FREQ_SPAN * 2.0 * fraction / TIMES
    forward = time_weight[None, :] * np.cos(frequency[:, None] * times_grid[None, :])
    backward = (
        2.0 / math.pi * freq_weight[None, :] * np.cos(times_grid[:, None] * frequency[None, :])
    )
    return forward.astype(np.float32), backward.astype(np.float32)


def forward_blocks(groups):
    forward, _ = transform_tables()
    whole = np.kron(np.eye(groups, dtype=np.float32), forward)
    high = whole.astype(ml_dtypes.bfloat16)
    low = (whole - high.astype(np.float32)).astype(ml_dtypes.bfloat16)
    return np.concatenate([high, low], axis=1)


def kernel(
    sizes,
    rows_hbm, cols_hbm, slab_hbm, occ_ref, virt_ref, coulomb_hbm, forward_ref, backward_ref,
    out_hbm,
    raw, rows, decay, scaled0, scaled1, own_scaled, cols, coulomb, slab, chi, freq,
    half, half_send, half_recv, sum_send, sum_recv, mine, green, sigma,
    raw_sem, cols_sem, misc_sem, half_ssem, half_rsem, sum_ssem, sum_rsem, out_ssem, out_rsem,
    own_sem,
):
    teams, zs, ys, share, band = sizes
    owners = zs * ys * CORES
    peers = zs * ys
    tiles = cols.shape[0]
    orbitals = decay.shape[1]
    chunk = owners * TIMES
    halves = chunk // CORES
    strip = orbitals // tiles
    t = lax.axis_index("tm")
    p = lax.axis_index("pts")
    core = lax.rem(p, CORES)
    y = lax.rem(p // CORES, ys)
    z = p // (CORES * ys)
    partner = (t, p + 1 - 2 * core)

    def peer(h):
        return lax.rem(z + h // ys, zs), lax.rem(y + h % ys, ys)

    def peer_id(h):
        pz, py = peer(h)
        return (t, (pz * ys + py) * CORES + core)

    def team_id(d):
        return (lax.rem(t + d, teams), p)

    barrier = pltpu.get_barrier_semaphore()
    pl.semaphore_signal(barrier, inc=1, device_id=partner, device_id_type=MESH)
    for h in range(1, peers):
        pl.semaphore_signal(barrier, inc=1, device_id=peer_id(h), device_id_type=MESH)
    for d in range(1, teams):
        pl.semaphore_signal(barrier, inc=1, device_id=team_id(d), device_id_type=MESH)

    def raw_copy(g):
        pz, py = peer(g % peers)
        owner = (pz * ys + py) * CORES + (1 - core if g < peers else core)
        first = pl.multiple_of(owner * (teams * share) + (t * share) // band * band, band)
        return pltpu.make_async_copy(
            rows_hbm.at[pl.ds(first, band)], raw.at[pl.ds(g * band, band)], raw_sem.at[g]
        )

    def cols_copy(n):
        return pltpu.make_async_copy(
            cols_hbm.at[:, pl.ds(pl.multiple_of(n * TILE, TILE), TILE)], cols.at[n], cols_sem.at[n]
        )

    for g in range(owners):
        raw_copy(g).start()
    for n in range(tiles):
        cols_copy(n).start()
    coulomb_copy = pltpu.make_async_copy(coulomb_hbm, coulomb, misc_sem.at[0])
    slab_copy = pltpu.make_async_copy(slab_hbm, slab, misc_sem.at[1])
    coulomb_copy.start()
    slab_copy.start()

    fraction = (lax.broadcasted_iota(jnp.int32, (TIMES, 1), 0).astype(jnp.float32) + 0.5) / TIMES
    moments = TIME_SPAN * fraction * fraction
    decay[:, :NOCC] = jnp.exp(-occ_ref[...] * moments)
    decay[:, NOCC:] = jnp.exp(-virt_ref[...] * moments)
    for g in range(owners):
        raw_copy(g).wait()
    rows[...] = raw[...].astype(jnp.float32)
    inner = lax.rem(t * share, band)

    def scale(target, s, n):
        where = pl.ds(pl.multiple_of(n * strip, strip), strip)
        factor = decay[:, where]
        for g in range(owners):
            row = rows[pl.ds(g * band + inner + s, 1), where]
            target[g * TIMES : (g + 1) * TIMES, where] = (row * factor).astype(jnp.bfloat16)

    scaled = (scaled0, scaled1)
    own_group = peers
    for s in range(share):
        row = rows[pl.ds(own_group * band + inner + s, 1), :NOCC]
        own_scaled[s * TIMES : (s + 1) * TIMES] = (row * decay[:, :NOCC]).astype(jnp.bfloat16)

    def first_scale(n, carry):
        scale(scaled0, 0, n)
        return carry

    lax.fori_loop(0, tiles, first_scale, 0)

    def half_copy(s):
        return pltpu.make_async_remote_copy(
            half_send.at[s], half_recv.at[s], half_ssem.at[s], half_rsem.at[s],
            device_id=partner, device_id_type=MESH,
        )

    def sum_copy(s, h):
        return pltpu.make_async_remote_copy(
            sum_send.at[s, pl.ds(h * TIMES, TIMES)], sum_recv.at[s, h - 1], sum_ssem.at[s, h - 1],
            sum_rsem.at[s, h - 1], device_id=peer_id(h), device_id_type=MESH,
        )

    def out_copy(s, d):
        return pltpu.make_async_remote_copy(
            sigma.at[s, lax.rem(t + d, teams)], out_hbm.at[t * share + s],
            out_ssem.at[s, d - 1], out_rsem.at[s, d - 1],
            device_id=team_id(d), device_id_type=MESH,
        )

    def own_copy(s):
        return pltpu.make_async_copy(sigma.at[s, t], out_hbm.at[t * share + s], own_sem.at[s])

    def green_loop(s, between):
        now, later = scaled[s % 2], scaled[(s + 1) % 2]

        def body(n, carry):
            if s == 0:
                cols_copy(n).wait()
            occ = jnp.dot(now[:, :NOCC], cols[n, :NOCC], preferred_element_type=jnp.float32)
            virt = jnp.dot(now[:, NOCC:], cols[n, NOCC:], preferred_element_type=jnp.float32)
            where = pl.ds(pl.multiple_of(n * TILE, TILE), TILE)
            chi[:, where] = (occ * virt).astype(jnp.bfloat16)
            if s + 1 < share:
                scale(later, s + 1, n)
            for after, work in between.items():
                pl.when(n == after)(work)
            return carry

        lax.fori_loop(0, tiles, body, 0)

    def screen(s):
        for n in range(chi.shape[1] // TILE):
            where = slice(n * TILE, (n + 1) * TILE)
            for part in range(CORES):
                group = slice(part * halves, (part + 1) * halves)
                twice = jnp.concatenate([chi[group, where]] * 2, axis=0)
                freq[group, where] = jnp.dot(
                    forward_ref[...], twice, preferred_element_type=jnp.float32
                ).astype(jnp.bfloat16)
        if s == 0:
            coulomb_copy.wait()
        for n in range(coulomb.shape[1] // TILE):
            where = slice(n * TILE, (n + 1) * TILE)
            part = jnp.dot(freq[...], coulomb[:, where], preferred_element_type=jnp.float32)
            half_send[s, :, where] = part[:halves].astype(jnp.bfloat16)
            half[:, where] = part[halves:]
        if s == 0:
            pl.semaphore_wait(barrier, 1 + (peers - 1) + (teams - 1))
        half_copy(s).start()

    def pair_up(s):
        half_copy(s).wait_recv()
        total = half[...] + half_recv[s].astype(jnp.float32)
        sum_send[s] = total.astype(jnp.bfloat16)
        mine[s] = total[:TIMES]
        for h in range(peers - 1, 0, -1):
            sum_copy(s, h).start()

    def slab_part():
        slab_copy.wait()
        green[...] = jnp.dot(own_scaled[...], slab[...], preferred_element_type=jnp.float32)

    def finish(s):
        for h in range(1, peers):
            sum_copy(s, h).wait_recv()
        total = mine[s]
        for h in range(1, peers):
            total = total + sum_recv[s, h - 1].astype(jnp.float32)
        resummed = total / jnp.sqrt(1.0 + total * total)
        by_time = jnp.dot(
            backward_ref[...], resummed, preferred_element_type=jnp.float32,
            precision=lax.Precision.HIGHEST,
        )
        result = by_time * green[s * TIMES : (s + 1) * TIMES]
        local = TIMES // teams
        for d in range(teams):
            sigma[s, d] = result[d * local : (d + 1) * local]
        for d in range(teams - 1, 0, -1):
            out_copy(s, d).start()
        own_copy(s).start()

    for s in range(share):
        between = {}
        if s > 0:
            between[0] = functools.partial(pair_up, s - 1)
        if s > 1:
            between[1] = functools.partial(finish, s - 2)
        green_loop(s, between)
        if s == 0:
            slab_part()
        screen(s)
    pair_up(share - 1)
    for s in range(max(share - 2, 0), share):
        finish(s)
    for s in range(share):
        half_copy(s).wait_send()
        for h in range(1, peers):
            sum_copy(s, h).wait_send()
        own_copy(s).wait()
        for d in range(1, teams):
            out_copy(s, d).wait_send()
            out_copy(s, d).wait_recv()


def per_device(sizes, psi_rows, psi_cols, psi_slab, occ_depth, virt_height, coulomb):
    teams, zs, ys, share, band = sizes
    owners = zs * ys * CORES
    peers = zs * ys
    orbitals = psi_rows.shape[1]
    points = psi_cols.shape[1]
    slab = psi_slab.shape[1]
    chunk = owners * TIMES
    halves = chunk // CORES
    _, backward = transform_tables()
    bf16, f32 = jnp.bfloat16, jnp.float32
    anywhere = pl.BlockSpec(memory_space=pl.ANY)
    inside = pl.BlockSpec(memory_space=pltpu.VMEM)
    dma = pltpu.SemaphoreType.DMA
    return pl.pallas_call(
        functools.partial(kernel, sizes),
        name="gw_window",
        out_shape=jax.ShapeDtypeStruct((teams * share, TIMES // teams, slab), f32),
        in_specs=[anywhere, anywhere, anywhere, inside, inside, anywhere, inside, inside],
        out_specs=anywhere,
        scratch_shapes=[
            pltpu.VMEM((owners * band, orbitals), bf16),
            pltpu.VMEM((owners * band, orbitals), f32),
            pltpu.VMEM((TIMES, orbitals), f32),
            pltpu.VMEM((chunk, orbitals), bf16),
            pltpu.VMEM((chunk, orbitals), bf16),
            pltpu.VMEM((share * TIMES, NOCC), bf16),
            pltpu.VMEM((points // TILE, orbitals, TILE), bf16),
            pltpu.VMEM((points, slab), bf16),
            pltpu.VMEM((NOCC, slab), bf16),
            pltpu.VMEM((chunk, points), bf16),
            pltpu.VMEM((chunk, points), bf16),
            pltpu.VMEM((halves, slab), f32),
            pltpu.VMEM((share, halves, slab), bf16),
            pltpu.VMEM((share, halves, slab), bf16),
            pltpu.VMEM((share, halves, slab), bf16),
            pltpu.VMEM((share, peers - 1, TIMES, slab), bf16),
            pltpu.VMEM((share, TIMES, slab), f32),
            pltpu.VMEM((share * TIMES, slab), f32),
            pltpu.VMEM((share, teams, TIMES // teams, slab), f32),
            dma((owners,)),
            dma((points // TILE,)),
            dma((2,)),
            dma((share,)),
            dma((share,)),
            dma((share, peers - 1)),
            dma((share, peers - 1)),
            dma((share, teams - 1)),
            dma((share, teams - 1)),
            dma((share,)),
        ],
        compiler_params=pltpu.CompilerParams(
            collective_id=0, has_side_effects=True, vmem_limit_bytes=60 * 1024 * 1024
        ),
    )(
        psi_rows, psi_cols, psi_slab, occ_depth[None], virt_height[None], coulomb,
        jnp.asarray(forward_blocks(peers)), jnp.asarray(backward),
    )


def solution(mesh):
    teams, owners = mesh.shape["tm"], mesh.shape["pts"]
    ys = owners // (2 * CORES)
    sizes = (teams, 2, ys, 512 // (owners * teams), 8)
    in_specs = (P(), P(None, "pts"), P(), P(), P(), P("pts", None))
    out_specs = P("pts", "tm", None)
    return jax.shard_map(
        functools.partial(per_device, sizes),
        mesh=mesh, in_specs=in_specs, out_specs=out_specs, check_vma=False,
    )
```

```python
import functools
import math

import jax
import jax.numpy as jnp
import ml_dtypes
import numpy as np
from jax import lax
from jax.experimental import pallas as pl
from jax.experimental.pallas import tpu as pltpu
from jax.sharding import PartitionSpec as P

MESH = pl.DeviceIdType.MESH
NOCC = 1024
TIMES = 16
TIME_SPAN = 8.0
FREQ_SPAN = 8.0
TILE = 256
CORES = 2


def transform_tables():
    fraction = (np.arange(TIMES, dtype=np.float64) + 0.5) / TIMES
    times_grid = TIME_SPAN * fraction * fraction
    time_weight = TIME_SPAN * 2.0 * fraction / TIMES
    frequency = FREQ_SPAN * fraction * fraction
    freq_weight = FREQ_SPAN * 2.0 * fraction / TIMES
    forward = time_weight[None, :] * np.cos(frequency[:, None] * times_grid[None, :])
    backward = (
        2.0 / math.pi * freq_weight[None, :] * np.cos(times_grid[:, None] * frequency[None, :])
    )
    return forward.astype(np.float32), backward.astype(np.float32)


def forward_blocks(groups):
    forward, _ = transform_tables()
    whole = np.kron(np.eye(groups, dtype=np.float32), forward)
    high = whole.astype(ml_dtypes.bfloat16)
    low = (whole - high.astype(np.float32)).astype(ml_dtypes.bfloat16)
    return np.concatenate([high, low], axis=1)


def kernel(
    sizes,
    rows_hbm, cols_hbm, slab_hbm, occ_hbm, virt_hbm, coulomb_hbm, forward_hbm, backward_hbm,
    out_hbm,
    raw, rows, decay, scaled0, scaled1, own_scaled, cols, coulomb, slab, chi, freq,
    half, half_send, half_recv, sum_send, sum_recv, mine, green, sigma, depth, forward, backward,
    raw_sem, cols_sem, misc_sem, half_ssem, half_rsem, sum_ssem, sum_rsem, out_ssem, out_rsem,
    own_sem,
):
    teams, zs, ys, share, band = sizes
    owners = zs * ys * CORES
    peers = zs * ys
    tiles = cols.shape[0]
    orbitals = decay.shape[1]
    chunk = owners * TIMES
    halves = chunk // CORES
    strip = orbitals // tiles
    t = lax.axis_index("tm")
    p = lax.axis_index("pts")
    core = lax.rem(p, CORES)
    y = lax.rem(p // CORES, ys)
    z = p // (CORES * ys)
    partner = (t, p + 1 - 2 * core)

    def peer(h):
        return lax.rem(z + h // ys, zs), lax.rem(y + h % ys, ys)

    def peer_id(h):
        pz, py = peer(h)
        return (t, (pz * ys + py) * CORES + core)

    def team_id(d):
        return (lax.rem(t + d, teams), p)

    barrier = pltpu.get_barrier_semaphore()
    pl.semaphore_signal(barrier, inc=1, device_id=partner, device_id_type=MESH)
    for h in range(1, peers):
        pl.semaphore_signal(barrier, inc=1, device_id=peer_id(h), device_id_type=MESH)
    for d in range(1, teams):
        pl.semaphore_signal(barrier, inc=1, device_id=team_id(d), device_id_type=MESH)

    def raw_copy(g):
        pz, py = peer(g % peers)
        owner = (pz * ys + py) * CORES + (1 - core if g < peers else core)
        first = pl.multiple_of(owner * (teams * share) + (t * share) // band * band, band)
        return pltpu.make_async_copy(
            rows_hbm.at[pl.ds(first, band)], raw.at[pl.ds(g * band, band)], raw_sem.at[g]
        )

    def cols_copy(n):
        return pltpu.make_async_copy(
            cols_hbm.at[:, pl.ds(pl.multiple_of(n * TILE, TILE), TILE)], cols.at[n], cols_sem.at[n]
        )

    small_copies = [
        pltpu.make_async_copy(occ_hbm, depth.at[:, pl.ds(0, NOCC)], misc_sem.at[2]),
        pltpu.make_async_copy(virt_hbm, depth.at[:, pl.ds(NOCC, orbitals - NOCC)], misc_sem.at[3]),
        pltpu.make_async_copy(forward_hbm, forward, misc_sem.at[4]),
        pltpu.make_async_copy(backward_hbm, backward, misc_sem.at[5]),
    ]
    for copy in small_copies:
        copy.start()
    for g in range(owners):
        raw_copy(g).start()
    cols_copy(0).start()
    coulomb_copy = pltpu.make_async_copy(coulomb_hbm, coulomb, misc_sem.at[0])
    slab_copy = pltpu.make_async_copy(slab_hbm, slab, misc_sem.at[1])

    fraction = (lax.broadcasted_iota(jnp.int32, (TIMES, 1), 0).astype(jnp.float32) + 0.5) / TIMES
    moments = TIME_SPAN * fraction * fraction
    for copy in small_copies:
        copy.wait()
    decay[...] = jnp.exp(-depth[...] * moments)
    for g in range(owners):
        raw_copy(g).wait()
    cols_copy(1).start()
    rows[...] = raw[...].astype(jnp.float32)
    inner = lax.rem(t * share, band)

    def scale(target, s, n):
        where = pl.ds(pl.multiple_of(n * strip, strip), strip)
        factor = decay[:, where]
        for g in range(owners):
            row = rows[pl.ds(g * band + inner + s, 1), where]
            target[g * TIMES : (g + 1) * TIMES, where] = (row * factor).astype(jnp.bfloat16)

    scaled = (scaled0, scaled1)
    def first_scale(n, carry):
        scale(scaled0, 0, n)
        return carry

    lax.fori_loop(0, tiles, first_scale, 0)

    def half_copy(s):
        return pltpu.make_async_remote_copy(
            half_send.at[s], half_recv.at[s], half_ssem.at[s], half_rsem.at[s],
            device_id=partner, device_id_type=MESH,
        )

    def sum_copy(s, h):
        return pltpu.make_async_remote_copy(
            sum_send.at[s, pl.ds(h * TIMES, TIMES)], sum_recv.at[s, h - 1], sum_ssem.at[s, h - 1],
            sum_rsem.at[s, h - 1], device_id=peer_id(h), device_id_type=MESH,
        )

    def out_copy(s, d):
        return pltpu.make_async_remote_copy(
            sigma.at[s, lax.rem(t + d, teams)], out_hbm.at[t * share + s],
            out_ssem.at[s, d - 1], out_rsem.at[s, d - 1],
            device_id=team_id(d), device_id_type=MESH,
        )

    def own_copy(s):
        return pltpu.make_async_copy(sigma.at[s, t], out_hbm.at[t * share + s], own_sem.at[s])

    def green_tile(now, n):
        occ = jnp.dot(now[:, :NOCC], cols[n, :NOCC], preferred_element_type=jnp.float32)
        virt = jnp.dot(now[:, NOCC:], cols[n, NOCC:], preferred_element_type=jnp.float32)
        where = pl.ds(pl.multiple_of(n * TILE, TILE), TILE)
        chi[:, where] = (occ * virt).astype(jnp.bfloat16)

    def first_green():
        def body(n, carry):
            cols_copy(n).wait()

            @pl.when(n + 2 < tiles)
            def _():
                cols_copy(n + 2).start()

            pl.when(n == tiles - 2)(coulomb_copy.start)
            pl.when(n == tiles - 1)(slab_copy.start)
            green_tile(scaled0, n)
            scale(scaled1, 1, n)
            return carry

        lax.fori_loop(0, tiles, body, 0)

    def green_loop(s):
        now, later = scaled[s % 2], scaled[(s + 1) % 2]

        def body(pair, carry):
            for n in (2 * pair, 2 * pair + 1):
                green_tile(now, n)
                if s + 1 < share:
                    scale(later, s + 1, n)
            pl.when(pair == 0)(functools.partial(pair_up, s - 1))
            return carry

        lax.fori_loop(0, tiles // 2, body, 0)

    def screen(s):
        for n in range(chi.shape[1] // TILE):
            where = slice(n * TILE, (n + 1) * TILE)
            for part in range(CORES):
                group = slice(part * halves, (part + 1) * halves)
                twice = jnp.concatenate([chi[group, where]] * 2, axis=0)
                freq[group, where] = jnp.dot(
                    forward[...], twice, preferred_element_type=jnp.float32
                ).astype(jnp.bfloat16)
        if s == 0:
            coulomb_copy.wait()
        for n in range(coulomb.shape[1] // TILE):
            where = slice(n * TILE, (n + 1) * TILE)
            part = jnp.dot(freq[...], coulomb[:, where], preferred_element_type=jnp.float32)
            half_send[s, :, where] = part[:halves].astype(jnp.bfloat16)
            half[:, where] = part[halves:]
        if s == 0:
            pl.semaphore_wait(barrier, 1 + (peers - 1) + (teams - 1))
        half_copy(s).start()

    def pair_up(s):
        half_copy(s).wait_recv()
        total = half[...] + half_recv[s].astype(jnp.float32)
        sum_send[s] = total.astype(jnp.bfloat16)
        mine[s] = total[:TIMES]
        for h in range(peers - 1, 0, -1):
            sum_copy(s, h).start()

    def slab_part():
        slab_copy.wait()
        for s in range(share):
            row = rows[pl.ds(peers * band + inner + s, 1), :NOCC]
            own_scaled[s * TIMES : (s + 1) * TIMES] = (row * decay[:, :NOCC]).astype(jnp.bfloat16)
        green[...] = jnp.dot(own_scaled[...], slab[...], preferred_element_type=jnp.float32)

    def finish(s):
        for h in range(1, peers):
            sum_copy(s, h).wait_recv()
        total = mine[s]
        for h in range(1, peers):
            total = total + sum_recv[s, h - 1].astype(jnp.float32)
        resummed = total / jnp.sqrt(1.0 + total * total)
        by_time = jnp.dot(
            backward[...], resummed, preferred_element_type=jnp.float32,
            precision=lax.Precision.HIGHEST,
        )
        result = by_time * green[s * TIMES : (s + 1) * TIMES]
        local = TIMES // teams
        for d in range(teams):
            sigma[s, d] = result[d * local : (d + 1) * local]
        for d in range(teams - 1, 0, -1):
            out_copy(s, d).start()
        own_copy(s).start()

    first_green()
    screen(0)
    for s in range(1, share):
        green_loop(s)
        if s == 1:
            slab_part()
        if 1 < s < share - 1:
            finish(s - 2)
        screen(s)
    pair_up(share - 1)
    for s in range(max(share - 3, 0), share):
        finish(s)
    for s in range(share):
        half_copy(s).wait_send()
        for h in range(1, peers):
            sum_copy(s, h).wait_send()
        own_copy(s).wait()
        for d in range(1, teams):
            out_copy(s, d).wait_send()
            out_copy(s, d).wait_recv()


def per_device(sizes, psi_rows, psi_cols, psi_slab, occ_depth, virt_height, coulomb):
    teams, zs, ys, share, band = sizes
    owners = zs * ys * CORES
    peers = zs * ys
    orbitals = psi_rows.shape[1]
    points = psi_cols.shape[1]
    slab = psi_slab.shape[1]
    chunk = owners * TIMES
    halves = chunk // CORES
    _, to_times = transform_tables()
    bf16, f32 = jnp.bfloat16, jnp.float32
    outside = pl.BlockSpec(memory_space=pltpu.HBM)
    dma = pltpu.SemaphoreType.DMA
    return pl.pallas_call(
        functools.partial(kernel, sizes),
        name="gw_window",
        out_shape=jax.ShapeDtypeStruct((teams * share, TIMES // teams, slab), f32),
        in_specs=[outside] * 8,
        out_specs=pl.BlockSpec(memory_space=pl.ANY),
        scratch_shapes=[
            pltpu.VMEM((owners * band, orbitals), bf16),
            pltpu.VMEM((owners * band, orbitals), f32),
            pltpu.VMEM((TIMES, orbitals), f32),
            pltpu.VMEM((chunk, orbitals), bf16),
            pltpu.VMEM((chunk, orbitals), bf16),
            pltpu.VMEM((share * TIMES, NOCC), bf16),
            pltpu.VMEM((points // TILE, orbitals, TILE), bf16),
            pltpu.VMEM((points, slab), bf16),
            pltpu.VMEM((NOCC, slab), bf16),
            pltpu.VMEM((chunk, points), bf16),
            pltpu.VMEM((chunk, points), bf16),
            pltpu.VMEM((halves, slab), f32),
            pltpu.VMEM((share, halves, slab), bf16),
            pltpu.VMEM((share, halves, slab), bf16),
            pltpu.VMEM((share, halves, slab), bf16),
            pltpu.VMEM((share, peers - 1, TIMES, slab), bf16),
            pltpu.VMEM((share, TIMES, slab), f32),
            pltpu.VMEM((share * TIMES, slab), f32),
            pltpu.VMEM((share, teams, TIMES // teams, slab), f32),
            pltpu.VMEM((1, orbitals), f32),
            pltpu.VMEM((halves, CORES * halves), bf16),
            pltpu.VMEM((TIMES, TIMES), f32),
            dma((owners,)),
            dma((points // TILE,)),
            dma((6,)),
            dma((share,)),
            dma((share,)),
            dma((share, peers - 1)),
            dma((share, peers - 1)),
            dma((share, teams - 1)),
            dma((share, teams - 1)),
            dma((share,)),
        ],
        compiler_params=pltpu.CompilerParams(
            collective_id=0, has_side_effects=True, vmem_limit_bytes=53 * 1024 * 1024
        ),
    )(
        psi_rows, psi_cols, psi_slab, occ_depth[None], virt_height[None], coulomb,
        jnp.asarray(forward_blocks(peers)), jnp.asarray(to_times),
    )


def solution(mesh):
    teams, owners = mesh.shape["tm"], mesh.shape["pts"]
    ys = owners // (2 * CORES)
    sizes = (teams, 2, ys, 512 // (owners * teams), 8)
    in_specs = (P(), P(None, "pts"), P(), P(), P(), P("pts", None))
    out_specs = P("pts", "tm", None)
    return jax.shard_map(
        functools.partial(per_device, sizes),
        mesh=mesh, in_specs=in_specs, out_specs=out_specs, check_vma=False,
    )
```
